256 devices in a mesh: seq: 128 (over z, y, x_lo, core), head: 2 (over x_hi).
Axes of the slice: x: 4 (x_hi: 2, x_lo: 2; x = x_hi * 2 + x_lo), y: 4, z: 8, core: 2. Of those that a mesh axis runs over, the one named last changes fastest.
Arguments:
- queries: bfloat16 [32768, 4096], P('seq', 'head'), may hold values from -8 to 8
- keys: bfloat16 [32768, 2048], P('seq', 'head'), may hold values from -8 to 8
- values: bfloat16 [32768, 2048], P('seq', 'head'), may hold values from -6 to 6
- segment_ids: int32 [32768], P(('seq', 'head')), may hold values from 0 to 63, never falling along the last dimension, each value on 1 to 2048 neighbouring positions
Outputs:
- attended: bfloat16 [32768, 4096], P('seq', 'head')
The draws below stay inside these ranges and needn't reach their ends.
Inputs may be any that keep to these rules, and one draw needn't show every extreme that they name: `segment_ids`: document numbers never fall along the tokens; each document has 1 to 2048 tokens, one exactly 2048.
All inputs are finite; a program needn't handle non-finite values.
Results may differ from the reference program's by a relative error of at most 0.0037.
Values may be sent and summed in bfloat16 or wider, within the bound.
A program may use at most 64 MiB of HBM per device.

```python
import math
import jax
import jax.numpy as jnp
import numpy as np
from jax import lax

HQ = 32
KEY_VALUE_HEADS = 16
HEAD_WIDTH = 128
WINDOW = 1024
TOK_DEV = 256
MOST = 2048
PACKED_TOKENS = 32768
COUNT = 64
N_SEQ = 128


def draw_queries(key, part):
    final_output = jnp.clip(jax.random.normal(jax.random.fold_in(key, 1), (PACKED_TOKENS, HQ * HEAD_WIDTH)), -8.0, 8.0)
    return final_output.astype(jnp.bfloat16)


def draw_keys(key, part):
    final_output = jnp.clip(jax.random.normal(jax.random.fold_in(key, 2), (PACKED_TOKENS, KEY_VALUE_HEADS * HEAD_WIDTH)), -8.0, 8.0)
    return final_output.astype(jnp.bfloat16)


def block_scale(rng, dims, shards, smallest, largest):
    gain = 1.0
    for dim, shards_of in shards:
        draws = jax.random.uniform(jax.random.fold_in(jax.random.fold_in(rng, 6), dim), (shards_of,), jnp.float32, smallest / len(shards), largest / len(shards))
        gain = gain * jnp.repeat(jnp.exp(draws), dims[dim] // shards_of).reshape((-1,) + (1,) * (len(dims) - 1 - dim))
    return gain


def length_profile(count, total, reach, skew):
    loads = [(1 << 20) // math.isqrt(grade ** skew) + 1 for grade in range(2, count + 1)]
    rest, holding = total - reach - (count - 1), [1] * (count - 1)
    while rest > 0:
        candidates = [i for i in range(count - 1) if holding[i] < reach]
        whole, remaining = sum([loads[i] for i in candidates]), rest
        for i in candidates:
            addition = min(reach - holding[i], max(1, remaining * loads[i] // whole), rest)
            holding[i] = holding[i] + addition
            rest = rest - addition
    return np.array([reach] + holding)


def ragged(own_key, count, total, limit, lean):
    if count == 2:
        one = jax.random.randint(own_key, (), max(1, total - limit), min(limit, total - 1) + 1)
        return jnp.stack([one, total - one])
    sizes = jnp.asarray(length_profile(count, total, limit, lean), jnp.int32)
    twos = (count - 1) // 2
    donor, taker = sizes[1:1 + 2 * twos:2], sizes[2:2 + 2 * twos:2]
    margin = jnp.minimum(donor - 1, limit - taker)
    moved = jax.random.randint(jax.random.fold_in(own_key, 1), (twos,), 0, 1 << 20) % (margin + 1)
    sizes = sizes.at[1:1 + 2 * twos:2].set(donor - moved).at[2:2 + 2 * twos:2].set(taker + moved)
    return sizes[jax.random.permutation(jax.random.fold_in(own_key, 2), count)]


def scatter_about(rng, dims, spread, limit, split=(), kind=jnp.bfloat16):
    result = spread * jax.random.normal(rng, dims, jnp.float32)
    if split:
        result = result * block_scale(rng, dims, split, -0.22, 0.18)
    return jnp.clip(result, -limit, limit).astype(kind)


def setup_inputs(seed: int = 0) -> dict:
    arg_keys = jax.random.split(jax.random.key(seed), 5)
    queries = draw_queries(jax.random.fold_in(arg_keys[4], 71), 0)
    keys = draw_keys(jax.random.fold_in(arg_keys[4], 71), 0)
    values = scatter_about(arg_keys[2], (PACKED_TOKENS, KEY_VALUE_HEADS * HEAD_WIDTH), 1.0, 6.0, ((0, 128), (1, 2)))
    segment_ids = jnp.searchsorted(jnp.cumsum(ragged(arg_keys[3], COUNT, PACKED_TOKENS, MOST, 2)), jnp.arange(PACKED_TOKENS), side="right").astype(jnp.int32)
    return {"queries": queries, "keys": keys, "values": values, "segment_ids": segment_ids}


score_scale = 168.0 ** -0.5


def attend(queries, keys, values, query_ids, key_ids, query_pos, key_pos):
    tok_rows = queries.shape[0]
    span = keys.shape[0]
    kv_heads = keys.shape[1] // HEAD_WIDTH
    group = queries.shape[1] // keys.shape[1]
    visible = (key_ids[None, :] == query_ids[:, None]) & (key_pos[None, :] <= query_pos[:, None]) & (query_pos[:, None] - key_pos[None, :] < WINDOW)
    grouped_q = queries.reshape(tok_rows, kv_heads, group, HEAD_WIDTH).transpose(1, 0, 2, 3)
    grouped_k = keys.reshape(span, kv_heads, HEAD_WIDTH).transpose(1, 0, 2)
    grouped_v = values.reshape(span, kv_heads, HEAD_WIDTH).transpose(1, 0, 2)

    def one_head(operands):
        head_q, head_k, head_v = operands
        scores = jnp.einsum('tgd,sd->gts', head_q.astype(jnp.float32), head_k.astype(jnp.float32)) * score_scale
        scores = jnp.where(visible[None], scores, -1e30)
        top = jnp.max(scores, axis=2, keepdims=True)
        weights = jnp.exp(scores - top)
        total = jnp.sum(weights, axis=2)
        rounded = weights.astype(jnp.bfloat16)
        mixed = jnp.einsum('gts,sd->tgd', rounded.astype(jnp.float32), head_v.astype(jnp.float32))
        return (mixed / total.T[:, :, None]).astype(jnp.bfloat16)

    final_output = lax.map(one_head, (grouped_q, grouped_k, grouped_v))
    return final_output.transpose(1, 0, 2, 3).reshape(tok_rows, -1)


def reference(queries, keys, values, segment_ids):
    padded_k = jnp.concatenate([jnp.zeros((WINDOW, keys.shape[1]), keys.dtype), keys])
    padded_v = jnp.concatenate([jnp.zeros((WINDOW, values.shape[1]), values.dtype), values])
    padded_ids = jnp.concatenate([jnp.full((WINDOW,), -1, jnp.int32), segment_ids.astype(jnp.int32)])
    span = WINDOW + TOK_DEV
    query_pos = jnp.arange(TOK_DEV, dtype=jnp.int32)
    key_pos = jnp.arange(span, dtype=jnp.int32) - WINDOW

    def block(index):
        start = (index * TOK_DEV).astype(jnp.int32)
        block_q = lax.dynamic_slice_in_dim(queries, start, TOK_DEV, 0)
        block_ids = lax.dynamic_slice_in_dim(segment_ids.astype(jnp.int32), start, TOK_DEV, 0)
        block_k = lax.dynamic_slice_in_dim(padded_k, start, span, 0)
        block_v = lax.dynamic_slice_in_dim(padded_v, start, span, 0)
        key_ids = lax.dynamic_slice_in_dim(padded_ids, start, span, 0)
        return attend(block_q, block_k, block_v, block_ids, key_ids, query_pos, key_pos)

    final_output = lax.map(block, jnp.arange(N_SEQ, dtype=jnp.int32))
    return final_output.reshape(PACKED_TOKENS, -1)
```

```python
import functools

import jax
import jax.numpy as jnp
from jax import lax
from jax.experimental import pallas as pl
from jax.experimental.pallas import tpu as pltpu
from jax.sharding import PartitionSpec as P

HEAD_WIDTH = 128
WINDOW = 1024
SCALE = 168.0 ** (-0.5)
LOG2E = 1.4426950408889634
MESH = pl.DeviceIdType.MESH


def kernel(n_seq, q_hbm, k_hbm, v_hbm, id_hbm, out_hbm,
           kv, qbuf, obuf, ids, bias, p_buf, l_buf,
           ld_sem, q_sem, o_sem, id_sem, id_send, id_recv,
           y_send, y_recv, x_send, x_recv, a_send, b_send, c1_recv, c3_recv):
    rows = k_hbm.shape[0]
    heads = k_hbm.shape[1] // HEAD_WIDTH
    half = id_hbm.shape[1]
    span = kv.shape[2]
    s = lax.axis_index("seq")
    head = lax.axis_index("head")
    core = lax.rem(s, 2)
    chip = lax.rem(s // 2, 2)
    y_next = (lax.rem(s + 4, n_seq), head)
    y_prev = (lax.rem(s + n_seq - 4, n_seq), head)
    x_peer = (s + 2 - 4 * chip, head)
    c_peer = (s + 1 - 2 * core, head)
    h_peer = (s, 1 - head)

    x_src = 4 * (1 - chip)
    a_src, a_dst = 4 * (1 - core), 3 - 2 * core
    b_dst = 1 + 2 * core

    def part(c, h, slot):
        return kv.at[c, h, pl.ds(pl.multiple_of(slot * rows, rows), rows), :]

    def load(c, h, ref):
        return pltpu.make_async_copy(
            ref.at[:, pl.ds(pl.multiple_of(h * HEAD_WIDTH, HEAD_WIDTH), HEAD_WIDTH)],
            part(c, h, 4), ld_sem.at[c, h])

    def load_q(h):
        return pltpu.make_async_copy(
            q_hbm.at[:, pl.ds(pl.multiple_of(h * 256, 256), 256)], qbuf.at[h], q_sem.at[h])

    def store(h):
        return pltpu.make_async_copy(
            obuf.at[h], out_hbm.at[:, pl.ds(pl.multiple_of(h * 256, 256), 256)], o_sem.at[h])

    def remote(src, dst, send, recv, dev):
        return pltpu.make_async_remote_copy(
            src_ref=src, dst_ref=dst, send_sem=send, recv_sem=recv,
            device_id=dev, device_id_type=MESH)

    def y_copy(c, h):
        return remote(part(c, h, 4), part(c, h, 0), y_send.at[c, h], y_recv.at[c, h], y_next)

    def x_copy(c, h):
        return remote(part(c, h, x_src), part(c, h, 2), x_send.at[c, h], x_recv.at[c, h], x_peer)

    def a_copy(c, h):
        return remote(part(c, h, a_src), part(c, h, a_dst), a_send.at[c, h],
                      c1_recv.at[c, h], c_peer)

    def b_copy(c, h):
        return remote(part(c, h, 2), part(c, h, b_dst), b_send.at[c, h],
                      c3_recv.at[c, h], c_peer)

    own_id = pltpu.make_async_copy(id_hbm, ids.at[head, 4], id_sem)
    own_id.start()

    @pl.loop(0, heads)
    def _(h):
        load(0, h, k_hbm).start()
        load(1, h, v_hbm).start()

    @pl.loop(0, heads)
    def _(h):
        load_q(h).start()

    barrier = pltpu.get_barrier_semaphore()
    for peer in (y_next, y_prev, x_peer, c_peer, h_peer):
        pl.semaphore_signal(barrier, inc=1, device_id=peer, device_id_type=MESH)
    own_id.wait()
    pl.semaphore_wait(barrier, 5)

    id_y = remote(ids.at[head, 4], ids.at[head, 0], id_send.at[0], id_recv.at[0], y_next)
    id_y.start()

    @pl.loop(0, heads)
    def _(h):
        load(0, h, k_hbm).wait()
        y_copy(0, h).start()
        load(1, h, v_hbm).wait()
        y_copy(1, h).start()

    id_x = remote(ids.at[head, x_src], ids.at[head, 2], id_send.at[1], id_recv.at[1], x_peer)
    id_a = remote(ids.at[head, a_src], ids.at[head, a_dst], id_send.at[2], id_recv.at[2], c_peer)
    id_b = remote(ids.at[head, 2], ids.at[head, b_dst], id_send.at[3], id_recv.at[3], c_peer)
    id_h = remote(ids.at[head], ids.at[head], id_send.at[4], id_recv.at[4], h_peer)
    id_y.wait_recv()
    id_x.start()
    id_a.start()
    id_x.wait_recv()
    id_b.start()
    id_a.wait_recv()
    id_b.wait_recv()
    id_h.start()

    def relay_y(c, h):
        y_copy(c, h).wait_recv()
        x_copy(c, h).start()
        a_copy(c, h).start()

    def relay_x(c, h):
        x_copy(c, h).wait_recv()
        b_copy(c, h).start()

    def arrive(c, h):
        remote(part(c, h, 4), part(c, h, 1), a_send.at[c, h], c1_recv.at[c, h], c_peer).wait_recv()
        remote(part(c, h, 4), part(c, h, 1), a_send.at[c, h], c3_recv.at[c, h], c_peer).wait_recv()

    def make_bias():
        own = [
            jnp.swapaxes(jnp.broadcast_to(ids[t, 4], (half, half)), 0, 1)
            for t in range(2)
        ]
        row = lax.broadcasted_iota(jnp.int32, (half, half), 0)
        lane = lax.broadcasted_iota(jnp.int32, (half, half), 1)
        for top in range(2):
            for slot in range(5):
                for t in range(2):
                    key_pos = slot * rows + t * half - 4 * rows
                    gap = row + (top * half - key_pos) - lane
                    visible = (
                        (own[top] == ids[t, slot])
                        & (gap >= 0) & (gap < WINDOW)
                        & (lane + (s * rows + key_pos) >= 0)
                    )
                    bias[pl.ds(top * half, half), pl.ds(slot * rows + t * half, half)] = (
                        jnp.where(visible, 0.0, -1e30)
                    )

    def weigh(h):
        load_q(h).wait()
        for t in range(2):
            scores = lax.dot_general(
                qbuf[h, :, pl.ds(t * HEAD_WIDTH, HEAD_WIDTH)], kv[0, h],
                (((1,), (1,)), ((), ())), preferred_element_type=jnp.float32)
            scores = scores * (SCALE * LOG2E) + bias[...]
            top = jnp.max(scores, axis=1, keepdims=True)
            weights = jnp.exp2(scores - top)
            l_buf[t] = jnp.broadcast_to(jnp.sum(weights, axis=1, keepdims=True), (rows, HEAD_WIDTH))
            p_buf[t] = weights.astype(jnp.bfloat16)

    def mix(h):
        for t in range(2):
            mixed = jnp.dot(p_buf[t], kv[1, h], preferred_element_type=jnp.float32)
            obuf[h, :, pl.ds(t * HEAD_WIDTH, HEAD_WIDTH)] = (mixed / l_buf[t]).astype(jnp.bfloat16)
        store(h).start()

    @pl.loop(0, heads + 1)
    def _(h):
        @pl.when(h < heads)
        def _():
            relay_y(0, h)

        @pl.when(h >= 1)
        def _():
            relay_x(1, h - 1)
            arrive(0, h - 1)

            @pl.when(h == 1)
            def _():
                id_h.wait_recv()
                make_bias()

            weigh(h - 1)

        @pl.when(h < heads)
        def _():
            relay_y(1, h)
            relay_x(0, h)

        @pl.when(h >= 1)
        def _():
            arrive(1, h - 1)
            mix(h - 1)

    for copy in (id_y, id_x, id_a, id_b, id_h):
        copy.wait_send()

    @pl.loop(0, heads)
    def _(h):
        for c in range(2):
            y_copy(c, h).wait_send()
            x_copy(c, h).wait_send()
            a_copy(c, h).wait_send()
            b_copy(c, h).wait_send()
        store(h).wait()


def body(queries, keys, values, segment_ids):
    rows, width = keys.shape
    heads = width // HEAD_WIDTH
    n_seq = lax.axis_size("seq")
    half = segment_ids.shape[0]
    dma = pltpu.SemaphoreType.DMA
    return pl.pallas_call(
        functools.partial(kernel, n_seq),
        out_shape=jax.ShapeDtypeStruct(queries.shape, queries.dtype),
        in_specs=[pl.BlockSpec(memory_space=pl.ANY)] * 4,
        out_specs=pl.BlockSpec(memory_space=pl.ANY),
        scratch_shapes=[
            pltpu.VMEM((2, heads, 5 * rows, HEAD_WIDTH), jnp.bfloat16),
            pltpu.VMEM((heads, rows, 256), jnp.bfloat16),
            pltpu.VMEM((heads, rows, 256), jnp.bfloat16),
            pltpu.VMEM((2, 5, 1, half), jnp.int32),
            pltpu.VMEM((rows, 5 * rows), jnp.float32),
            pltpu.VMEM((2, rows, 5 * rows), jnp.bfloat16),
            pltpu.VMEM((2, rows, HEAD_WIDTH), jnp.float32),
            dma((2, heads)), dma((heads,)), dma((heads,)), dma, dma((5,)), dma((5,)),
            dma((2, heads)), dma((2, heads)), dma((2, heads)), dma((2, heads)),
            dma((2, heads)), dma((2, heads)), dma((2, heads)), dma((2, heads)),
        ],
        compiler_params=pltpu.CompilerParams(collective_id=0, has_side_effects=True),
    )(queries, keys, values, segment_ids.reshape(1, half))


def solution(mesh):
    in_specs = (P("seq", "head"), P("seq", "head"), P("seq", "head"), P(("seq", "head")))
    out_specs = P("seq", "head")
    return jax.shard_map(body, mesh=mesh, in_specs=in_specs, out_specs=out_specs, check_vma=False)
```

```python
import functools

import jax
import jax.numpy as jnp
from jax import lax
from jax.experimental import pallas as pl
from jax.experimental.pallas import tpu as pltpu
from jax.sharding import PartitionSpec as P

HEAD_WIDTH = 128
WINDOW = 1024
SCALE = 168.0 ** (-0.5)
LOG2E = 1.4426950408889634
MESH = pl.DeviceIdType.MESH
X_LAG = 3


def kernel(n_seq, q_hbm, k_hbm, v_hbm, id_hbm, out,
           kv, qbuf, ids, bias, p_buf, l_buf,
           ld_sem, q_sem, id_sem, id_send, id_recv,
           y_send, y_recv, x_send, x_recv, a_send, b_send, c1_recv, c3_recv):
    rows = k_hbm.shape[0]
    heads = k_hbm.shape[1] // HEAD_WIDTH
    half = id_hbm.shape[1]
    span = kv.shape[2]
    s = lax.axis_index("seq")
    head = lax.axis_index("head")
    core = lax.rem(s, 2)
    chip = lax.rem(s // 2, 2)
    y_next = (lax.rem(s + 4, n_seq), head)
    y_prev = (lax.rem(s + n_seq - 4, n_seq), head)
    x_peer = (s + 2 - 4 * chip, head)
    c_peer = (s + 1 - 2 * core, head)
    h_peer = (s, 1 - head)

    x_src = 4 * (1 - chip)
    a_src, a_dst = 4 * (1 - core), 3 - 2 * core
    b_dst = 1 + 2 * core

    def part(c, h, slot):
        return kv.at[c, h, pl.ds(pl.multiple_of(slot * rows, rows), rows), :]

    def load(c, h, ref):
        return pltpu.make_async_copy(
            ref.at[:, pl.ds(pl.multiple_of(h * HEAD_WIDTH, HEAD_WIDTH), HEAD_WIDTH)],
            part(c, h, 4), ld_sem.at[c, h])

    def load_q(h):
        return pltpu.make_async_copy(
            q_hbm.at[:, pl.ds(pl.multiple_of(h * 256, 256), 256)], qbuf.at[h], q_sem.at[h])

    def remote(src, dst, send, recv, dev):
        return pltpu.make_async_remote_copy(
            src_ref=src, dst_ref=dst, send_sem=send, recv_sem=recv,
            device_id=dev, device_id_type=MESH)

    def y_copy(c, h):
        return remote(part(c, h, 4), part(c, h, 0), y_send.at[c, h], y_recv.at[c, h], y_next)

    def x_copy(c, h):
        return remote(part(c, h, x_src), part(c, h, 2), x_send.at[c, h], x_recv.at[c, h], x_peer)

    def a_copy(c, h):
        return remote(part(c, h, a_src), part(c, h, a_dst), a_send.at[c, h],
                      c1_recv.at[c, h], c_peer)

    def b_copy(c, h):
        return remote(part(c, h, 2), part(c, h, b_dst), b_send.at[c, h],
                      c3_recv.at[c, h], c_peer)

    first = s < 4
    last = s >= n_seq - 4
    steps = 2 * heads

    def split(i):
        return lax.rem(i, 2), i // 2

    def fill(c, h, ref):
        return pltpu.make_async_copy(
            ref.at[:, pl.ds(pl.multiple_of(h * HEAD_WIDTH, HEAD_WIDTH), HEAD_WIDTH)],
            part(c, h, 0), y_recv.at[c, h])

    own_id = pltpu.make_async_copy(id_hbm, ids.at[head, 4], id_sem)
    own_id.start()

    @pl.loop(0, heads)
    def _(h):
        load(0, h, k_hbm).start()
        load(1, h, v_hbm).start()

    barrier = pltpu.get_barrier_semaphore()
    for peer in (x_peer, c_peer, h_peer):
        pl.semaphore_signal(barrier, inc=1, device_id=peer, device_id_type=MESH)

    @pl.when(jnp.logical_not(first))
    def _():
        pl.semaphore_signal(barrier, inc=1, device_id=y_prev, device_id_type=MESH)

    @pl.when(jnp.logical_not(last))
    def _():
        pl.semaphore_signal(barrier, inc=1, device_id=y_next, device_id_type=MESH)

    @pl.loop(0, heads)
    def _(h):
        load_q(h).start()

    @pl.when(first)
    def _():
        pltpu.make_async_copy(id_hbm, ids.at[head, 0], id_recv.at[0]).start()

        @pl.loop(0, heads)
        def _(h):
            fill(0, h, k_hbm).start()
            fill(1, h, v_hbm).start()

    own_id.wait()
    pl.semaphore_wait(barrier, 5 - first.astype(jnp.int32) - last.astype(jnp.int32))

    id_y = remote(ids.at[head, 4], ids.at[head, 0], id_send.at[0], id_recv.at[0], y_next)
    id_x = remote(ids.at[head, x_src], ids.at[head, 2], id_send.at[1], id_recv.at[1], x_peer)
    id_a = remote(ids.at[head, a_src], ids.at[head, a_dst], id_send.at[2], id_recv.at[2], c_peer)
    id_b = remote(ids.at[head, 2], ids.at[head, b_dst], id_send.at[3], id_recv.at[3], c_peer)
    id_h = remote(ids.at[head], ids.at[head], id_send.at[4], id_recv.at[4], h_peer)

    @pl.when(jnp.logical_not(last))
    def _():
        id_y.start()

    @pl.loop(0, heads)
    def _(h):
        load(0, h, k_hbm).wait()
        load(1, h, v_hbm).wait()

        @pl.when(jnp.logical_not(last))
        def _():
            y_copy(0, h).start()
            y_copy(1, h).start()

    id_y.wait_recv()
    id_x.start()
    id_a.start()

    def relay_y(i):
        c, h = split(i)
        y_copy(c, h).wait_recv()
        x_copy(c, h).start()
        a_copy(c, h).start()

    def relay_x(i):
        c, h = split(i)
        x_copy(c, h).wait_recv()
        b_copy(c, h).start()

    def arrive(c, h):
        a_copy(c, h).wait_recv()
        b_copy(c, h).wait_recv()

    def make_bias():
        own = [
            jnp.swapaxes(jnp.broadcast_to(ids[t, 4], (half, half)), 0, 1)
            for t in range(2)
        ]
        row = lax.broadcasted_iota(jnp.int32, (half, half), 0)
        lane = lax.broadcasted_iota(jnp.int32, (half, half), 1)
        for top in range(2):
            for slot in range(5):
                for t in range(2):
                    key_pos = slot * rows + t * half - 4 * rows
                    gap = row + (top * half - key_pos) - lane
                    visible = (
                        (own[top] == ids[t, slot])
                        & (gap >= 0) & (gap < WINDOW)
                        & (lane + (s * rows + key_pos) >= 0)
                    )
                    bias[pl.ds(top * half, half), pl.ds(slot * rows + t * half, half)] = (
                        jnp.where(visible, 0.0, -1e30)
                    )

    def weigh(h):
        load_q(h).wait()
        for t in range(2):
            scores = lax.dot_general(
                qbuf[h, :, pl.ds(t * HEAD_WIDTH, HEAD_WIDTH)], kv[0, h],
                (((1,), (1,)), ((), ())), preferred_element_type=jnp.float32)
            scores = scores * (SCALE * LOG2E) + bias[...]
            top = jnp.max(scores, axis=1, keepdims=True)
            weights = jnp.exp2(scores - top)
            l_buf[t] = jnp.broadcast_to(jnp.sum(weights, axis=1, keepdims=True), (rows, HEAD_WIDTH))
            p_buf[t] = weights.astype(jnp.bfloat16)

    def mix(h):
        for t in range(2):
            mixed = jnp.dot(p_buf[t], kv[1, h], preferred_element_type=jnp.float32)
            out[:, pl.ds(pl.multiple_of(h * 256 + t * HEAD_WIDTH, HEAD_WIDTH), HEAD_WIDTH)] = (
                mixed / l_buf[t]).astype(jnp.bfloat16)

    relay_y(0)
    relay_y(1)
    id_x.wait_recv()
    id_b.start()
    id_a.wait_recv()
    id_b.wait_recv()
    id_h.start()

    @pl.loop(1, heads + 2)
    def _(h):
        for c in range(2):
            i = 2 * h + c

            @pl.when(i < steps)
            def _():
                relay_y(i)

            @pl.when((i >= X_LAG) & (i < steps + X_LAG))
            def _():
                relay_x(i - X_LAG)

            @pl.when(h >= 2)
            def _():
                arrive(c, h - 2)
                if c == 0:
                    @pl.when(h == 2)
                    def _():
                        id_h.wait_recv()
                        make_bias()

                    weigh(h - 2)
                else:
                    mix(h - 2)

    for copy in (id_x, id_a, id_b, id_h):
        copy.wait_send()

    @pl.when(jnp.logical_not(last))
    def _():
        id_y.wait_send()

        @pl.loop(0, heads)
        def _(h):
            y_copy(0, h).wait_send()
            y_copy(1, h).wait_send()

    @pl.loop(0, heads)
    def _(h):
        for c in range(2):
            x_copy(c, h).wait_send()
            a_copy(c, h).wait_send()
            b_copy(c, h).wait_send()


def body(queries, keys, values, segment_ids):
    rows, width = keys.shape
    heads = width // HEAD_WIDTH
    n_seq = lax.axis_size("seq")
    half = segment_ids.shape[0]
    dma = pltpu.SemaphoreType.DMA
    return pl.pallas_call(
        functools.partial(kernel, n_seq),
        out_shape=pltpu.VMEM(queries.shape, queries.dtype),
        in_specs=[pl.BlockSpec(memory_space=pl.ANY)] * 4,
        out_specs=pl.BlockSpec(memory_space=pltpu.VMEM),
        scratch_shapes=[
            pltpu.VMEM((2, heads, 5 * rows, HEAD_WIDTH), jnp.bfloat16),
            pltpu.VMEM((heads, rows, 256), jnp.bfloat16),
            pltpu.VMEM((2, 5, 1, half), jnp.int32),
            pltpu.VMEM((rows, 5 * rows), jnp.float32),
            pltpu.VMEM((2, rows, 5 * rows), jnp.bfloat16),
            pltpu.VMEM((2, rows, HEAD_WIDTH), jnp.float32),
            dma((2, heads)), dma((heads,)), dma, dma((5,)), dma((5,)),
            dma((2, heads)), dma((2, heads)), dma((2, heads)), dma((2, heads)),
            dma((2, heads)), dma((2, heads)), dma((2, heads)), dma((2, heads)),
        ],
        compiler_params=pltpu.CompilerParams(collective_id=0, has_side_effects=True),
    )(queries, keys, values, segment_ids.reshape(1, half))


def solution(mesh):
    in_specs = (P("seq", "head"), P("seq", "head"), P("seq", "head"), P(("seq", "head")))
    out_specs = P("seq", "head")
    return jax.shard_map(body, mesh=mesh, in_specs=in_specs, out_specs=out_specs, check_vma=False)
```

```python
import functools

import jax
import jax.numpy as jnp
from jax import lax
from jax.experimental import pallas as pl
from jax.experimental.pallas import tpu as pltpu
from jax.sharding import PartitionSpec as P

HEAD_WIDTH = 128
WINDOW = 1024
SCALE = 168.0 ** (-0.5)
LOG2E = 1.4426950408889634
MESH = pl.DeviceIdType.MESH
X_LAG = 2
UNIT_LAG = 4
EARLY = 14
HELD = 13
AHEAD = 4


def kernel(n_seq, q_hbm, k_hbm, v_hbm, id_hbm, out,
           kv, early, qbuf, ids, bias, p_buf, l_buf,
           ld_sem, q_sem, id_sem, e_sem, id_send, id_recv,
           y_send, y_recv, x_send, x_recv, a_send, a_recv, b_send, b_recv):
    rows = k_hbm.shape[0]
    heads = k_hbm.shape[1] // HEAD_WIDTH
    half = id_hbm.shape[1]
    span = kv.shape[2]
    s = lax.axis_index("seq")
    head = lax.axis_index("head")
    core = lax.rem(s, 2)
    chip = lax.rem(s // 2, 2)
    y_next = (lax.rem(s + 4, n_seq), head)
    y_prev = (lax.rem(s + n_seq - 4, n_seq), head)
    x_peer = (s + 2 - 4 * chip, head)
    c_peer = (s + 1 - 2 * core, head)
    cross = (s + 2 - 4 * chip, 1 - head)

    x_src = 4 * (1 - chip)
    a_src, a_dst = 4 * (1 - core), 3 - 2 * core
    b_dst = 1 + 2 * core

    steps = 2 * heads

    def unit(i):
        c = 1 - lax.rem(i, 2) + i // (steps - 1) - (steps - 1 - i) // (steps - 1)
        return c, (i + 1) // 2 - c

    def chunk(i, slot):
        c, h = unit(i)
        return kv.at[c, h, pl.ds(pl.multiple_of(slot * rows, rows), rows), :]

    def columns(ref, h):
        return ref.at[:, pl.ds(pl.multiple_of(h * HEAD_WIDTH, HEAD_WIDTH), HEAD_WIDTH)]

    def own(i, slot, sem):
        return pltpu.make_async_copy(columns(k_hbm, 0), chunk(i, slot), sem.at[i])

    def start_own(i, slot, sem):
        c, h = unit(i)

        @pl.when(c == 0)
        def _():
            pltpu.make_async_copy(columns(k_hbm, h), chunk(i, slot), sem.at[i]).start()

        @pl.when(c == 1)
        def _():
            pltpu.make_async_copy(columns(v_hbm, h), chunk(i, slot), sem.at[i]).start()

    def load_q(h):
        return pltpu.make_async_copy(
            q_hbm.at[:, pl.ds(pl.multiple_of(h * 256, 256), 256)], qbuf.at[h], q_sem.at[h])

    def remote(src, dst, send, recv, dev):
        return pltpu.make_async_remote_copy(
            src_ref=src, dst_ref=dst, send_sem=send, recv_sem=recv,
            device_id=dev, device_id_type=MESH)

    def y_copy(i):
        return remote(chunk(i, 4), chunk(i, 0), y_send, y_recv.at[i], y_next)

    def x_copy(i, send=x_send):
        return remote(chunk(i, x_src), chunk(i, 2), send, x_recv.at[i], x_peer)

    def a_copy(i):
        return remote(chunk(i, a_src), chunk(i, a_dst), a_send, a_recv.at[i], c_peer)

    def b_copy(i):
        return remote(chunk(i, 2), chunk(i, b_dst), b_send, b_recv.at[i], c_peer)

    def early_x():
        return remote(chunk(EARLY, 4), early, x_send, e_sem.at[0], x_peer)

    def early_y():
        return remote(early, chunk(EARLY, 2), e_sem.at[1], x_recv.at[EARLY], y_next)

    first = s < 4
    last = s >= n_seq - 4
    def x_sends(i):
        return (i < steps) & ((chip == 0) | (i != EARLY))

    barrier = pltpu.get_barrier_semaphore()

    @pl.when(jnp.logical_not(first))
    def _():
        pl.semaphore_signal(barrier, inc=1, device_id=y_prev, device_id_type=MESH)

    @pl.when(jnp.logical_not(last))
    def _():
        pl.semaphore_signal(barrier, inc=1, device_id=y_next, device_id_type=MESH)

    for peer in (cross, x_peer, c_peer):
        pl.semaphore_signal(barrier, inc=1, device_id=peer, device_id_type=MESH)

    own_id = pltpu.make_async_copy(id_hbm, ids.at[head, core, chip, 1], id_sem)
    own_id.start()

    @pl.loop(0, steps)
    def _(i):
        start_own(i, 4, ld_sem)

    @pl.loop(0, heads)
    def _(h):
        load_q(h).start()

    @pl.when(first)
    def _():
        pltpu.make_async_copy(id_hbm, ids.at[head, core, chip, 0], id_recv.at[0]).start()

        @pl.loop(0, steps)
        def _(i):
            start_own(i, 0, y_recv)

    own_id.wait()
    pl.semaphore_wait(barrier, 5 - first.astype(jnp.int32) - last.astype(jnp.int32))

    def id_copy(n, src, dst, dev):
        return remote(src, dst, id_send.at[n], id_recv.at[n], dev)

    mine = ids.at[head, core, chip]
    id_y = id_copy(0, mine.at[1], mine.at[0], y_next)
    id_x = id_copy(1, mine, mine, x_peer)
    id_c = id_copy(2, ids.at[head, core], ids.at[head, core], c_peer)
    id_h = id_copy(3, ids.at[head], ids.at[head], cross)

    @pl.when(jnp.logical_not(last))
    def _():
        id_y.start()

    @pl.loop(0, HELD)
    def _(i):
        own(i, 4, ld_sem).wait()

        @pl.when(jnp.logical_not(last))
        def _():
            y_copy(i).start()

    @pl.loop(HELD, steps)
    def _(i):
        own(i, 4, ld_sem).wait()

    @pl.when(chip == 1)
    def _():
        early_x().start()

    @pl.when(chip == 0)
    def _():
        x_copy(0).start()

    id_y.wait_recv()
    id_x.start()

    @pl.when(chip == 0)
    def _():
        @pl.loop(1, AHEAD)
        def _(i):
            x_copy(i).start()

    def relay_y(i):
        y_copy(i).wait_recv()
        out_i = i + AHEAD * (1 - chip)

        @pl.when(x_sends(out_i))
        def _():
            x_copy(out_i).start()

        @pl.when((i == EARLY) & (chip == 1) & first)
        def _():
            x_copy(i, e_sem.at[2]).start()

        a_copy(i).start()

    def relay_x(i):
        x_copy(i).wait_recv()
        b_copy(i).start()

    def arrive(i):
        a_copy(i).wait_recv()
        b_copy(i).wait_recv()

    def ids_of(t, slot):
        place = 2 * chip + core + slot
        r = lax.rem(place, 4)
        return ids[t, lax.rem(r, 2), r // 2, place // 4]

    def make_bias():
        mine = [
            jnp.swapaxes(jnp.broadcast_to(ids_of(t, 4), (half, half)), 0, 1)
            for t in range(2)
        ]
        row = lax.broadcasted_iota(jnp.int32, (half, half), 0)
        lane = lax.broadcasted_iota(jnp.int32, (half, half), 1)
        for top in range(2):
            for slot in range(5):
                for t in range(2):
                    key_pos = slot * rows + t * half - 4 * rows
                    gap = row + (top * half - key_pos) - lane
                    visible = (
                        (mine[top] == ids_of(t, slot))
                        & (gap >= 0) & (gap < WINDOW)
                        & (lane + (s * rows + key_pos) >= 0)
                    )
                    bias[pl.ds(top * half, half), pl.ds(slot * rows + t * half, half)] = (
                        jnp.where(visible, 0.0, -1e30)
                    )

    def weigh(h):
        load_q(h).wait()
        for t in range(2):
            scores = lax.dot_general(
                qbuf[h, :, pl.ds(t * HEAD_WIDTH, HEAD_WIDTH)], kv[0, h],
                (((1,), (1,)), ((), ())), preferred_element_type=jnp.float32)
            scores = scores * (SCALE * LOG2E) + bias[...]
            top = jnp.max(scores, axis=1, keepdims=True)
            weights = jnp.exp2(scores - top)
            l_buf[lax.rem(h, 2), t] = jnp.broadcast_to(jnp.sum(weights, axis=1, keepdims=True), (rows, HEAD_WIDTH))
            p_buf[lax.rem(h, 2), t] = weights.astype(jnp.bfloat16)

    def mix(h):
        for t in range(2):
            mixed = jnp.dot(p_buf[lax.rem(h, 2), t], kv[1, h], preferred_element_type=jnp.float32)
            out[:, pl.ds(pl.multiple_of(h * 256 + t * HEAD_WIDTH, HEAD_WIDTH), HEAD_WIDTH)] = (
                mixed / l_buf[lax.rem(h, 2), t]).astype(jnp.bfloat16)

    def step(i, state):
        relayed, done = state
        relay_y(i)

        @pl.when(i == 0)
        def _():
            id_x.wait_recv()
            id_c.start()

            @pl.when(chip == 0)
            def _():
                early_x().wait_recv()

            @pl.when(jnp.logical_not(last))
            def _():
                @pl.when(chip == 0)
                def _():
                    early_y().start()

                @pl.loop(HELD, steps)
                def _(j):
                    y_copy(j).start()

        @pl.when(i == 1)
        def _():
            id_c.wait_recv()
            id_h.start()

        relay_to = jnp.maximum(i + 1 - X_LAG, 0) + i // (steps - 4) + i // (steps - 3)
        relay_to = relay_to + (X_LAG - 2) * (i // (steps - 2))
        done_to = (jnp.maximum(i + 1 - UNIT_LAG, 0) + i // (steps - 4) + i // (steps - 3)
                   + (UNIT_LAG - 2) * (i // (steps - 1)))

        @pl.loop(relayed, relay_to)
        def _(j):
            relay_x(j)

        @pl.loop(done, done_to)
        def _(j):
            arrive(j)
            c, h = unit(j)

            @pl.when(j == 0)
            def _():
                id_h.wait_recv()
                make_bias()

            @pl.when(c == 0)
            def _():
                weigh(h)

            @pl.when(c == 1)
            def _():
                mix(h)

        return relay_to, done_to

    lax.fori_loop(0, steps, step, (jnp.int32(0), jnp.int32(0)))

    def sent(sem, peer):
        shard = kv.at[:, :, pl.ds(4 * rows, rows), :]
        remote(shard, shard, sem, y_recv.at[0], peer).wait_send()

    for copy in (id_x, id_c, id_h):
        copy.wait_send()
    sent(x_send, x_peer)
    sent(a_send, c_peer)
    sent(b_send, c_peer)

    @pl.when(jnp.logical_not(last))
    def _():
        id_y.wait_send()
        sent(y_send, y_next)

        @pl.when(chip == 0)
        def _():
            early_y().wait_send()

    @pl.when((chip == 1) & first)
    def _():
        x_copy(EARLY, e_sem.at[2]).wait_send()


def body(queries, keys, values, segment_ids):
    rows, width = keys.shape
    heads = width // HEAD_WIDTH
    n_seq = lax.axis_size("seq")
    half = segment_ids.shape[0]
    steps = 2 * heads
    dma = pltpu.SemaphoreType.DMA
    return pl.pallas_call(
        functools.partial(kernel, n_seq),
        out_shape=pltpu.VMEM(queries.shape, queries.dtype),
        in_specs=[pl.BlockSpec(memory_space=pl.ANY)] * 4,
        out_specs=pl.BlockSpec(memory_space=pltpu.VMEM),
        scratch_shapes=[
            pltpu.VMEM((2, heads, 5 * rows, HEAD_WIDTH), jnp.bfloat16),
            pltpu.VMEM((rows, HEAD_WIDTH), jnp.bfloat16),
            pltpu.VMEM((heads, rows, 256), jnp.bfloat16),
            pltpu.VMEM((2, 2, 2, 2, 1, half), jnp.int32),
            pltpu.VMEM((rows, 5 * rows), jnp.float32),
            pltpu.VMEM((2, 2, rows, 5 * rows), jnp.bfloat16),
            pltpu.VMEM((2, 2, rows, HEAD_WIDTH), jnp.float32),
            dma((steps,)), dma((heads,)), dma, dma((3,)), dma((4,)), dma((4,)),
            dma, dma((steps,)), dma, dma((steps,)),
            dma, dma((steps,)), dma, dma((steps,)),
        ],
        compiler_params=pltpu.CompilerParams(collective_id=0, has_side_effects=True),
    )(queries, keys, values, segment_ids.reshape(1, half))


def solution(mesh):
    in_specs = (P("seq", "head"), P("seq", "head"), P("seq", "head"), P(("seq", "head")))
    out_specs = P("seq", "head")
    return jax.shard_map(body, mesh=mesh, in_specs=in_specs, out_specs=out_specs, check_vma=False)
```

```python
import functools

import jax
import jax.numpy as jnp
from jax import lax
from jax.experimental import pallas as pl
from jax.experimental.pallas import tpu as pltpu
from jax.sharding import PartitionSpec as P

HEAD_WIDTH = 128
WINDOW = 1024
SCALE = 168.0 ** (-0.5)
LOG2E = 1.4426950408889634
MESH = pl.DeviceIdType.MESH
X_LAG = 2
UNIT_LAG = 4
EARLY = 13
HELD = 12
AHEAD = 4


def kernel(n_seq, q_hbm, k_hbm, v_hbm, id_hbm, out,
           kv, early, qbuf, ids, bias, p_buf, l_buf,
           ld_sem, q_sem, id_sem, e_sem, id_send, id_recv,
           y_send, y_recv, x_send, x_recv, a_send, a_recv, b_send, b_recv):
    rows = k_hbm.shape[0]
    heads = k_hbm.shape[1] // HEAD_WIDTH
    half = id_hbm.shape[1]
    span = kv.shape[2]
    s = lax.axis_index("seq")
    head = lax.axis_index("head")
    core = lax.rem(s, 2)
    chip = lax.rem(s // 2, 2)
    y_next = (lax.rem(s + 4, n_seq), head)
    y_prev = (lax.rem(s + n_seq - 4, n_seq), head)
    x_peer = (s + 2 - 4 * chip, head)
    c_peer = (s + 1 - 2 * core, head)
    cross = (s + 2 - 4 * chip, 1 - head)

    x_src = 4 * (1 - chip)
    a_src, a_dst = 4 * (1 - core), 3 - 2 * core
    b_dst = 1 + 2 * core

    steps = 2 * heads

    def unit(i):
        c = 1 - lax.rem(i, 2) + i // (steps - 1) - (steps - 1 - i) // (steps - 1)
        return c, (i + 1) // 2 - c

    def chunk(i, slot):
        c, h = unit(i)
        return kv.at[c, h, pl.ds(pl.multiple_of(slot * rows, rows), rows), :]

    def columns(ref, h):
        return ref.at[:, pl.ds(pl.multiple_of(h * HEAD_WIDTH, HEAD_WIDTH), HEAD_WIDTH)]

    def own(i, slot, sem):
        return pltpu.make_async_copy(columns(k_hbm, 0), chunk(i, slot), sem.at[i])

    def start_own(i, slot, sem):
        c, h = unit(i)

        @pl.when(c == 0)
        def _():
            pltpu.make_async_copy(columns(k_hbm, h), chunk(i, slot), sem.at[i]).start()

        @pl.when(c == 1)
        def _():
            pltpu.make_async_copy(columns(v_hbm, h), chunk(i, slot), sem.at[i]).start()

    def load_q(h):
        return pltpu.make_async_copy(
            q_hbm.at[:, pl.ds(pl.multiple_of(h * 256, 256), 256)], qbuf.at[h], q_sem.at[h])

    def remote(src, dst, send, recv, dev):
        return pltpu.make_async_remote_copy(
            src_ref=src, dst_ref=dst, send_sem=send, recv_sem=recv,
            device_id=dev, device_id_type=MESH)

    def y_copy(i):
        return remote(chunk(i, 4), chunk(i, 0), y_send, y_recv.at[i], y_next)

    def x_copy(i, send=x_send):
        return remote(chunk(i, x_src), chunk(i, 2), send, x_recv.at[i], x_peer)

    def a_copy(i):
        return remote(chunk(i, a_src), chunk(i, a_dst), a_send, a_recv.at[i], c_peer)

    def b_copy(i):
        return remote(chunk(i, 2), chunk(i, b_dst), b_send, b_recv.at[i], c_peer)

    def early_x():
        return remote(chunk(EARLY, 4), early, x_send, e_sem.at[0], x_peer)

    def early_y():
        return remote(early, chunk(EARLY, 2), e_sem.at[1], x_recv.at[EARLY], y_next)

    first = s < 4
    last = s >= n_seq - 4
    def x_sends(i):
        return (i < steps) & ((chip == 0) | (i != EARLY))

    barrier = pltpu.get_barrier_semaphore()

    @pl.when(jnp.logical_not(first))
    def _():
        pl.semaphore_signal(barrier, inc=1, device_id=y_prev, device_id_type=MESH)

    @pl.when(jnp.logical_not(last))
    def _():
        pl.semaphore_signal(barrier, inc=1, device_id=y_next, device_id_type=MESH)

    for peer in (cross, x_peer, c_peer):
        pl.semaphore_signal(barrier, inc=1, device_id=peer, device_id_type=MESH)

    own_id = pltpu.make_async_copy(id_hbm, ids.at[head, core, chip, 1], id_sem)
    own_id.start()

    @pl.loop(0, steps)
    def _(i):
        start_own(i, 4, ld_sem)

    @pl.loop(0, heads)
    def _(h):
        load_q(h).start()

    @pl.when(first)
    def _():
        pltpu.make_async_copy(id_hbm, ids.at[head, core, chip, 0], id_recv.at[0]).start()

        @pl.loop(0, steps)
        def _(i):
            start_own(i, 0, y_recv)

    own_id.wait()
    pl.semaphore_wait(barrier, 5 - first.astype(jnp.int32) - last.astype(jnp.int32))

    def id_copy(n, src, dst, dev):
        return remote(src, dst, id_send.at[n], id_recv.at[n], dev)

    mine = ids.at[head, core, chip]
    id_y = id_copy(0, mine.at[1], mine.at[0], y_next)
    id_x = id_copy(1, mine, mine, x_peer)
    id_c = id_copy(2, ids.at[head, core], ids.at[head, core], c_peer)
    id_h = id_copy(3, ids.at[head], ids.at[head], cross)

    @pl.when(jnp.logical_not(last))
    def _():
        id_y.start()

    @pl.loop(0, HELD)
    def _(i):
        own(i, 4, ld_sem).wait()

        @pl.when(jnp.logical_not(last))
        def _():
            y_copy(i).start()

    @pl.loop(HELD, steps)
    def _(i):
        own(i, 4, ld_sem).wait()

    @pl.when(chip == 1)
    def _():
        early_x().start()

    @pl.when(chip == 0)
    def _():
        x_copy(0).start()

    id_y.wait_recv()
    id_x.start()

    @pl.when(chip == 0)
    def _():
        @pl.loop(1, AHEAD)
        def _(i):
            x_copy(i).start()

    def relay_y(i):
        y_copy(i).wait_recv()
        out_i = i + AHEAD * (1 - chip)

        @pl.when(x_sends(out_i))
        def _():
            x_copy(out_i).start()

        @pl.when((i == EARLY) & (chip == 1) & first)
        def _():
            x_copy(i, e_sem.at[2]).start()

        a_copy(i).start()

    def relay_x(i):
        x_copy(i).wait_recv()
        b_copy(i).start()

    def arrive(i):
        a_copy(i).wait_recv()
        b_copy(i).wait_recv()

    def ids_of(t, slot):
        place = 2 * chip + core + slot
        r = lax.rem(place, 4)
        return ids[t, lax.rem(r, 2), r // 2, place // 4]

    def make_bias():
        mine = [
            jnp.swapaxes(jnp.broadcast_to(ids_of(t, 4), (half, half)), 0, 1)
            for t in range(2)
        ]
        row = lax.broadcasted_iota(jnp.int32, (half, half), 0)
        lane = lax.broadcasted_iota(jnp.int32, (half, half), 1)
        for top in range(2):
            for slot in range(5):
                for t in range(2):
                    key_pos = slot * rows + t * half - 4 * rows
                    gap = row + (top * half - key_pos) - lane
                    visible = (
                        (mine[top] == ids_of(t, slot))
                        & (gap >= 0) & (gap < WINDOW)
                        & (lane + (s * rows + key_pos) >= 0)
                    )
                    bias[pl.ds(top * half, half), pl.ds(slot * rows + t * half, half)] = (
                        jnp.where(visible, 0.0, -1e30)
                    )

    def weigh(h):
        load_q(h).wait()
        for t in range(2):
            scores = lax.dot_general(
                qbuf[h, :, pl.ds(t * HEAD_WIDTH, HEAD_WIDTH)], kv[0, h],
                (((1,), (1,)), ((), ())), preferred_element_type=jnp.float32)
            scores = scores * (SCALE * LOG2E) + bias[...]
            top = jnp.max(scores, axis=1, keepdims=True)
            weights = jnp.exp2(scores - top)
            l_buf[lax.rem(h, 2), t] = jnp.broadcast_to(jnp.sum(weights, axis=1, keepdims=True), (rows, HEAD_WIDTH))
            p_buf[lax.rem(h, 2), t] = weights.astype(jnp.bfloat16)

    def mix(h):
        for t in range(2):
            mixed = jnp.dot(p_buf[lax.rem(h, 2), t], kv[1, h], preferred_element_type=jnp.float32)
            out[:, pl.ds(pl.multiple_of(h * 256 + t * HEAD_WIDTH, HEAD_WIDTH), HEAD_WIDTH)] = (
                mixed / l_buf[lax.rem(h, 2), t]).astype(jnp.bfloat16)

    def step(i, state):
        relayed, done = state
        relay_y(i)

        @pl.when(i == 0)
        def _():
            id_x.wait_recv()
            id_c.start()

            @pl.when(chip == 0)
            def _():
                early_x().wait_recv()

            @pl.when(jnp.logical_not(last))
            def _():
                @pl.when(chip == 0)
                def _():
                    early_y().start()

                @pl.loop(HELD, steps)
                def _(j):
                    y_copy(j).start()

        @pl.when(i == 1)
        def _():
            id_c.wait_recv()
            id_h.start()

        relay_to = jnp.maximum(i + 1 - X_LAG, 0) + i // (steps - 4) + i // (steps - 3)
        relay_to = relay_to + (X_LAG - 2) * (i // (steps - 2))
        done_to = (jnp.maximum(i + 1 - UNIT_LAG, 0)
                   + (1 - chip) * (i // (steps - 6) + i // (steps - 3) - 2 * (i // (steps - 1)))
                   + UNIT_LAG * (i // (steps - 1)))

        @pl.loop(relayed, relay_to)
        def _(j):
            relay_x(j)

        @pl.loop(done, done_to)
        def _(j):
            arrive(j)
            c, h = unit(j)

            @pl.when(j == 0)
            def _():
                id_h.wait_recv()
                make_bias()

            @pl.when(c == 0)
            def _():
                weigh(h)

            @pl.when(c == 1)
            def _():
                mix(h)

        return relay_to, done_to

    lax.fori_loop(0, steps, step, (jnp.int32(0), jnp.int32(0)))

    def sent(sem, peer):
        shard = kv.at[:, :, pl.ds(4 * rows, rows), :]
        remote(shard, shard, sem, y_recv.at[0], peer).wait_send()

    for copy in (id_x, id_c, id_h):
        copy.wait_send()
    sent(x_send, x_peer)
    sent(a_send, c_peer)
    sent(b_send, c_peer)

    @pl.when(jnp.logical_not(last))
    def _():
        id_y.wait_send()
        sent(y_send, y_next)

        @pl.when(chip == 0)
        def _():
            early_y().wait_send()

    @pl.when((chip == 1) & first)
    def _():
        x_copy(EARLY, e_sem.at[2]).wait_send()


def body(queries, keys, values, segment_ids):
    rows, width = keys.shape
    heads = width // HEAD_WIDTH
    n_seq = lax.axis_size("seq")
    half = segment_ids.shape[0]
    steps = 2 * heads
    dma = pltpu.SemaphoreType.DMA
    return pl.pallas_call(
        functools.partial(kernel, n_seq),
        out_shape=pltpu.VMEM(queries.shape, queries.dtype),
        in_specs=[pl.BlockSpec(memory_space=pl.ANY)] * 4,
        out_specs=pl.BlockSpec(memory_space=pltpu.VMEM),
        scratch_shapes=[
            pltpu.VMEM((2, heads, 5 * rows, HEAD_WIDTH), jnp.bfloat16),
            pltpu.VMEM((rows, HEAD_WIDTH), jnp.bfloat16),
            pltpu.VMEM((heads, rows, 256), jnp.bfloat16),
            pltpu.VMEM((2, 2, 2, 2, 1, half), jnp.int32),
            pltpu.VMEM((rows, 5 * rows), jnp.float32),
            pltpu.VMEM((2, 2, rows, 5 * rows), jnp.bfloat16),
            pltpu.VMEM((2, 2, rows, HEAD_WIDTH), jnp.float32),
            dma((steps,)), dma((heads,)), dma, dma((3,)), dma((4,)), dma((4,)),
            dma, dma((steps,)), dma, dma((steps,)),
            dma, dma((steps,)), dma, dma((steps,)),
        ],
        compiler_params=pltpu.CompilerParams(collective_id=0, has_side_effects=True),
    )(queries, keys, values, segment_ids.reshape(1, half))


def solution(mesh):
    in_specs = (P("seq", "head"), P("seq", "head"), P("seq", "head"), P(("seq", "head")))
    out_specs = P("seq", "head")
    return jax.shard_map(body, mesh=mesh, in_specs=in_specs, out_specs=out_specs, check_vma=False)
```

```python
import functools

import jax
import jax.numpy as jnp
from jax import lax
from jax.experimental import pallas as pl
from jax.experimental.pallas import tpu as pltpu
from jax.sharding import PartitionSpec as P

HEAD_WIDTH = 128
WINDOW = 1024
SCALE = 168.0 ** (-0.5)
LOG2E = 1.4426950408889634
MESH = pl.DeviceIdType.MESH
X_LAG = 2
UNIT_LAG = 4
EARLY = 13
HELD = 12
AHEAD = 4


def kernel(n_seq, q_hbm, k_hbm, v_hbm, id_hbm, out,
           kv, early, qbuf, ids, bias, p_buf, l_buf,
           ld_sem, q_sem, id_sem, e_sem, id_send, id_recv,
           y_send, y_recv, x_send, x_recv, a_send, a_recv, b_send, b_recv):
    rows = k_hbm.shape[0]
    heads = k_hbm.shape[1] // HEAD_WIDTH
    half = id_hbm.shape[1]
    span = kv.shape[2]
    s = lax.axis_index("seq")
    head = lax.axis_index("head")
    core = lax.rem(s, 2)
    chip = lax.rem(s // 2, 2)
    y_next = (lax.rem(s + 4, n_seq), head)
    y_prev = (lax.rem(s + n_seq - 4, n_seq), head)
    x_peer = (s + 2 - 4 * chip, head)
    c_peer = (s + 1 - 2 * core, head)
    cross = (s + 2 - 4 * chip, 1 - head)

    x_src = 4 * (1 - chip)
    a_src, a_dst = 4 * (1 - core), 3 - 2 * core
    b_dst = 1 + 2 * core

    steps = 2 * heads

    def unit(i):
        c = 1 - lax.rem(i, 2) + i // (steps - 1) - (steps - 1 - i) // (steps - 1)
        return c, (i + 1) // 2 - c

    def chunk(i, slot):
        c, h = unit(i)
        return kv.at[c, h, pl.ds(pl.multiple_of(slot * rows, rows), rows), :]

    def columns(ref, h):
        return ref.at[:, pl.ds(pl.multiple_of(h * HEAD_WIDTH, HEAD_WIDTH), HEAD_WIDTH)]

    def own(i, slot, sem):
        return pltpu.make_async_copy(columns(k_hbm, 0), chunk(i, slot), sem.at[i])

    def start_own(i, slot, sem):
        c, h = unit(i)

        @pl.when(c == 0)
        def _():
            pltpu.make_async_copy(columns(k_hbm, h), chunk(i, slot), sem.at[i]).start()

        @pl.when(c == 1)
        def _():
            pltpu.make_async_copy(columns(v_hbm, h), chunk(i, slot), sem.at[i]).start()

    def load_q(h):
        return pltpu.make_async_copy(
            q_hbm.at[:, pl.ds(pl.multiple_of(h * 256, 256), 256)], qbuf.at[h], q_sem.at[h])

    def remote(src, dst, send, recv, dev):
        return pltpu.make_async_remote_copy(
            src_ref=src, dst_ref=dst, send_sem=send, recv_sem=recv,
            device_id=dev, device_id_type=MESH)

    def y_copy(i):
        return remote(chunk(i, 4), chunk(i, 0), y_send, y_recv.at[i], y_next)

    def x_copy(i, send=x_send):
        return remote(chunk(i, x_src), chunk(i, 2), send, x_recv.at[i], x_peer)

    def a_copy(i):
        return remote(chunk(i, a_src), chunk(i, a_dst), a_send, a_recv.at[i], c_peer)

    def b_copy(i):
        return remote(chunk(i, 2), chunk(i, b_dst), b_send, b_recv.at[i], c_peer)

    def early_x():
        return remote(chunk(EARLY, 4), early, x_send, e_sem.at[0], x_peer)

    def early_y():
        return remote(early, chunk(EARLY, 2), e_sem.at[1], x_recv.at[EARLY], y_next)

    first = s < 4
    last = s >= n_seq - 4
    def x_sends(i):
        return (i < steps) & ((chip == 0) | (i != EARLY))

    barrier = pltpu.get_barrier_semaphore()

    @pl.when(jnp.logical_not(first))
    def _():
        pl.semaphore_signal(barrier, inc=1, device_id=y_prev, device_id_type=MESH)

    @pl.when(jnp.logical_not(last))
    def _():
        pl.semaphore_signal(barrier, inc=1, device_id=y_next, device_id_type=MESH)

    for peer in (cross, x_peer, c_peer):
        pl.semaphore_signal(barrier, inc=1, device_id=peer, device_id_type=MESH)

    own_id = pltpu.make_async_copy(id_hbm, ids.at[head, core, chip, 1], id_sem)
    own_id.start()

    @pl.loop(0, steps)
    def _(i):
        start_own(i, 4, ld_sem)

    @pl.loop(0, heads)
    def _(h):
        load_q(h).start()

    @pl.when(first)
    def _():
        pltpu.make_async_copy(id_hbm, ids.at[head, core, chip, 0], id_recv.at[0]).start()

        @pl.loop(0, steps)
        def _(i):
            start_own(i, 0, y_recv)

    own_id.wait()
    pl.semaphore_wait(barrier, 5 - first.astype(jnp.int32) - last.astype(jnp.int32))

    def id_copy(n, src, dst, dev):
        return remote(src, dst, id_send.at[n], id_recv.at[n], dev)

    mine = ids.at[head, core, chip]
    id_y = id_copy(0, mine.at[1], mine.at[0], y_next)
    id_x = id_copy(1, mine, mine, x_peer)
    id_c = id_copy(2, ids.at[head, core], ids.at[head, core], c_peer)
    id_h = id_copy(3, ids.at[head], ids.at[head], cross)

    @pl.when(jnp.logical_not(last))
    def _():
        id_y.start()

    @pl.loop(0, HELD)
    def _(i):
        own(i, 4, ld_sem).wait()

        @pl.when(jnp.logical_not(last))
        def _():
            y_copy(i).start()

    @pl.loop(HELD, steps)
    def _(i):
        own(i, 4, ld_sem).wait()

    @pl.when(chip == 1)
    def _():
        early_x().start()

    @pl.when(chip == 0)
    def _():
        x_copy(0).start()

    id_y.wait_recv()
    id_x.start()

    @pl.when(chip == 0)
    def _():
        @pl.loop(1, AHEAD)
        def _(i):
            x_copy(i).start()

    def relay_y(i):
        y_copy(i).wait_recv()
        out_i = i + AHEAD * (1 - chip)

        @pl.when(x_sends(out_i))
        def _():
            x_copy(out_i).start()

        @pl.when((i == EARLY) & (chip == 1) & first)
        def _():
            x_copy(i, e_sem.at[2]).start()

        a_copy(i).start()

    def relay_x(i):
        x_copy(i).wait_recv()
        b_copy(i).start()

    def arrive(i):
        a_copy(i).wait_recv()
        b_copy(i).wait_recv()

    def ids_of(t, slot):
        place = 2 * chip + core + slot
        r = lax.rem(place, 4)
        return ids[t, lax.rem(r, 2), r // 2, place // 4]

    def make_bias():
        mine = [
            jnp.swapaxes(jnp.broadcast_to(ids_of(t, 4), (half, half)), 0, 1)
            for t in range(2)
        ]
        row = lax.broadcasted_iota(jnp.int32, (half, half), 0)
        lane = lax.broadcasted_iota(jnp.int32, (half, half), 1)
        for top in range(2):
            for slot in range(5):
                for t in range(2):
                    key_pos = slot * rows + t * half - 4 * rows
                    gap = row + (top * half - key_pos) - lane
                    visible = (
                        (mine[top] == ids_of(t, slot))
                        & (gap >= 0) & (gap < WINDOW)
                        & (lane + (s * rows + key_pos) >= 0)
                    )
                    bias[pl.ds(top * half, half), pl.ds(slot * rows + t * half, half)] = (
                        jnp.where(visible, 0.0, -1e30)
                    )

    def weigh(h):
        load_q(h).wait()
        for t in range(2):
            scores = lax.dot_general(
                qbuf[h, :, pl.ds(t * HEAD_WIDTH, HEAD_WIDTH)], kv[0, h],
                (((1,), (1,)), ((), ())), preferred_element_type=jnp.float32)
            scores = scores * (SCALE * LOG2E) + bias[...]
            top = jnp.max(scores, axis=1, keepdims=True)
            weights = jnp.exp2(scores - top)
            l_buf[lax.rem(h, 2), t] = jnp.broadcast_to(jnp.sum(weights, axis=1, keepdims=True), (rows, HEAD_WIDTH))
            p_buf[lax.rem(h, 2), t] = weights.astype(jnp.bfloat16)

    def mix(h):
        for t in range(2):
            mixed = jnp.dot(p_buf[lax.rem(h, 2), t], kv[1, h], preferred_element_type=jnp.float32)
            out[:, pl.ds(pl.multiple_of(h * 256 + t * HEAD_WIDTH, HEAD_WIDTH), HEAD_WIDTH)] = (
                mixed / l_buf[lax.rem(h, 2), t]).astype(jnp.bfloat16)

    def step(i, state):
        relayed, done = state
        relay_y(i)

        @pl.when(i == 0)
        def _():
            id_x.wait_recv()
            id_c.start()

            @pl.when(chip == 0)
            def _():
                early_x().wait_recv()

            @pl.when(jnp.logical_not(last))
            def _():
                @pl.when(chip == 0)
                def _():
                    early_y().start()

                @pl.loop(HELD, steps)
                def _(j):
                    y_copy(j).start()

        @pl.when(i == 1)
        def _():
            id_c.wait_recv()
            id_h.start()

        relay_to = jnp.maximum(i + 1 - X_LAG, 0) + i // (steps - 4) + i // (steps - 3)
        relay_to = relay_to + (X_LAG - 2) * (i // (steps - 2))
        done_to = (jnp.maximum(i + 1 - UNIT_LAG, 0)
                   + (1 - chip) * (i // (steps - 8) + i // (steps - 3) - 2 * (i // (steps - 1)))
                   + UNIT_LAG * (i // (steps - 1)))

        @pl.loop(relayed, relay_to)
        def _(j):
            relay_x(j)

        @pl.loop(done, done_to)
        def _(j):
            arrive(j)
            c, h = unit(j)

            @pl.when(j == 0)
            def _():
                id_h.wait_recv()
                make_bias()

            @pl.when(c == 0)
            def _():
                weigh(h)

            @pl.when(c == 1)
            def _():
                mix(h)

        return relay_to, done_to

    lax.fori_loop(0, steps, step, (jnp.int32(0), jnp.int32(0)))

    def sent(sem, peer):
        shard = kv.at[:, :, pl.ds(4 * rows, rows), :]
        remote(shard, shard, sem, y_recv.at[0], peer).wait_send()

    for copy in (id_x, id_c, id_h):
        copy.wait_send()
    sent(x_send, x_peer)
    sent(a_send, c_peer)
    sent(b_send, c_peer)

    @pl.when(jnp.logical_not(last))
    def _():
        id_y.wait_send()
        sent(y_send, y_next)

        @pl.when(chip == 0)
        def _():
            early_y().wait_send()

    @pl.when((chip == 1) & first)
    def _():
        x_copy(EARLY, e_sem.at[2]).wait_send()


def body(queries, keys, values, segment_ids):
    rows, width = keys.shape
    heads = width // HEAD_WIDTH
    n_seq = lax.axis_size("seq")
    half = segment_ids.shape[0]
    steps = 2 * heads
    dma = pltpu.SemaphoreType.DMA
    return pl.pallas_call(
        functools.partial(kernel, n_seq),
        out_shape=pltpu.VMEM(queries.shape, queries.dtype),
        in_specs=[pl.BlockSpec(memory_space=pl.ANY)] * 4,
        out_specs=pl.BlockSpec(memory_space=pltpu.VMEM),
        scratch_shapes=[
            pltpu.VMEM((2, heads, 5 * rows, HEAD_WIDTH), jnp.bfloat16),
            pltpu.VMEM((rows, HEAD_WIDTH), jnp.bfloat16),
            pltpu.VMEM((heads, rows, 256), jnp.bfloat16),
            pltpu.VMEM((2, 2, 2, 2, 1, half), jnp.int32),
            pltpu.VMEM((rows, 5 * rows), jnp.float32),
            pltpu.VMEM((2, 2, rows, 5 * rows), jnp.bfloat16),
            pltpu.VMEM((2, 2, rows, HEAD_WIDTH), jnp.float32),
            dma((steps,)), dma((heads,)), dma, dma((3,)), dma((4,)), dma((4,)),
            dma, dma((steps,)), dma, dma((steps,)),
            dma, dma((steps,)), dma, dma((steps,)),
        ],
        compiler_params=pltpu.CompilerParams(collective_id=0, has_side_effects=True),
    )(queries, keys, values, segment_ids.reshape(1, half))


def solution(mesh):
    in_specs = (P("seq", "head"), P("seq", "head"), P("seq", "head"), P(("seq", "head")))
    out_specs = P("seq", "head")
    return jax.shard_map(body, mesh=mesh, in_specs=in_specs, out_specs=out_specs, check_vma=False)
```
